32 devices in a mesh: view: 8 (over z, x), slab: 4 (over y, core).
Axes of the slice: x: 2, y: 2, z: 4, core: 2. Of those that a mesh axis runs over, the one named last changes fastest.
Arguments:
- volume: float32 [4, 128, 128], P('slab', 'view'), may hold values from 0 to 2
- tile_blocks: bfloat16 [8, 4, 192, 128, 128], P('view', 'slab'), may hold values from 0.0009994507 to 0.014953613
- pixel_tile: int32 [8, 4, 192], P('view', 'slab'), may hold values from 0 to 127, as said below
- ray_tile: int32 [8, 4, 192], P('view', 'slab'), may hold values from 0 to 127, as said below
- counts: int32 [8, 4], P('view', 'slab'), may hold values from 16 to 192, as said below
- subset_views: int32 [8, 4], P('view'), may hold values from 0 to 7, as said below
- sinogram: float32 [8, 128, 128], P('view', 'slab'), may hold values from 0 to 3
- weights: float32 [8, 128, 128], P('view', 'slab'), may hold values from 0.1 to 1
Outputs:
- updated: float32 [4, 128, 128], P('slab', 'view')
- denominators: float32 [4, 128, 128], P('slab', 'view')
The draws below stay inside these ranges and needn't reach their ends.
Inputs may be any that keep to these rules, and one draw needn't show every extreme that they name: `counts`: for every group exactly one slab has 192 live slots; every count is at least 16. `pixel_tile`: slots k < 16 of group g name volume tiles g * 16 + k in every slab; slots at or past the count hold indices in range and are unused. `ray_tile`: slots at or past the count hold indices in range and are unused. `subset_views`: each group lists 4 distinct views in rising order.
All inputs are finite; a program needn't handle non-finite values.
Results may differ from the reference program's by a relative error of at most 0.00032.
Values may be sent and summed in bfloat16 or wider, within the bound.
No kernel may reach another device: no remote copies, remote signals or barrier semaphores. Data moves between devices by JAX's collectives and lax.ppermute only.
A program may use at most 64 MiB of HBM per device.

```python
import math
from functools import partial
import jax
import jax.numpy as jnp
from jax import lax

TR = 128
TV = 128
K_MAX = 192
VT_DEV = 16
VG = 8
SUBSETS = 2
SV = 4
GROUPS = 8
SLABS = 4
VT = 128
RT = 128


def helix_pattern(key):
    base = jax.random.fold_in(key, 7)
    keys = jax.random.split(base, 4)
    centre = jax.random.randint(keys[0], (GROUPS,), 0, SLABS)
    slab_ids = jnp.arange(SLABS, dtype=jnp.int32)
    distance = jnp.abs(slab_ids[None, :] - centre[:, None])
    jitter = jax.random.randint(keys[1], (GROUPS, SLABS), 0, K_MAX // 8 + 1)
    far_count = jnp.maximum(VT_DEV, K_MAX // (2 * jnp.maximum(distance, 1)) - jitter)
    counts_out = jnp.where(distance == 0, K_MAX, far_count).astype(jnp.int32)
    random_pixels = jax.random.randint(keys[2], (GROUPS, SLABS, K_MAX), 0, VT)
    position = jnp.arange(K_MAX, dtype=jnp.int32)
    owned = jnp.arange(GROUPS, dtype=jnp.int32)[:, None, None] * VT_DEV + position[None, None, :]
    owned = jnp.broadcast_to(owned, (GROUPS, SLABS, K_MAX))
    pixels = jnp.where(position[None, None, :] < VT_DEV, owned, random_pixels).astype(jnp.int32)
    rays = jax.random.randint(keys[3], (GROUPS, SLABS, K_MAX), 0, RT).astype(jnp.int32)
    return (counts_out, pixels, rays)


def draw_counts(key, part):
    return helix_pattern(key)[0]


def draw_pixel_tile(key, part):
    return helix_pattern(key)[1]


def draw_ray_tile(key, part):
    return helix_pattern(key)[2]


def draw_subset_views(key, part):
    keys = jax.random.split(jax.random.fold_in(key, 11), GROUPS)

    def one_group(group_key):
        return jnp.sort(jax.random.permutation(group_key, VG)[:SV])
    return jax.vmap(one_group)(keys).astype(jnp.int32)


def block_scale(own_key, shape, cuts, low, largest):
    def one(dim, blocks):
        draws = jax.random.uniform(jax.random.fold_in(jax.random.fold_in(own_key, 6), dim), (blocks,), jnp.float32, low / len(cuts), largest / len(cuts))
        return jnp.repeat(jnp.exp(draws), shape[dim] // blocks).reshape((-1,) + (1,) * (len(shape) - dim - 1))

    factor_of = one(*cuts[0])
    for cut in cuts[1:]:
        factor_of = factor_of * one(*cut)
    return factor_of


def setup_inputs(seed: int = 0) -> dict:
    key_list = jax.random.split(jax.random.key(seed), 9)
    volume = jnp.clip(2.0 * jax.random.uniform(key_list[0], (SLABS, VT, TV), jnp.float32) ** block_scale(key_list[0], (SLABS, VT, TV), ((0, 4), (1, 8)), -0.2, 0.2), 0.0, 2.0)
    tile_blocks = jnp.clip(0.0009994507 + 0.013954163 * jax.random.uniform(key_list[1], (GROUPS, SLABS, K_MAX, TR, TV), jnp.float32) ** block_scale(key_list[1], (GROUPS, SLABS, K_MAX, TR, TV), ((0, 8), (1, 4)), -0.2, 0.2), 0.0009994507, 0.014953613).astype(jnp.bfloat16)
    pixel_tile = draw_pixel_tile(jax.random.fold_in(key_list[8], 71), 0)
    ray_tile = draw_ray_tile(jax.random.fold_in(key_list[8], 71), 0)
    counts = draw_counts(jax.random.fold_in(key_list[8], 71), 0)
    subset_views = draw_subset_views(jax.random.fold_in(key_list[8], 71), 0)
    sinogram = jnp.clip(3.0 * jax.random.uniform(key_list[6], (GROUPS, RT, TR), jnp.float32) ** block_scale(key_list[6], (GROUPS, RT, TR), ((0, 8), (1, 4)), -0.2, 0.2), 0.0, 3.0)
    weights = jnp.clip(jnp.exp(math.log(1.0) - 2.3025851 * jax.random.uniform(key_list[7], (GROUPS, RT, TR), jnp.float32) ** block_scale(key_list[7], (GROUPS, RT, TR), ((0, 8), (1, 4)), -0.2, 0.2)), 0.1, 1.0)
    return dict(volume=volume, tile_blocks=tile_blocks, pixel_tile=pixel_tile, ray_tile=ray_tile, counts=counts, subset_views=subset_views, sinogram=sinogram, weights=weights)


def forward_one(block_tiles, pixel_rows, ray_rows, count_here, slab_image, ray_total):
    live_mask = (jnp.arange(block_tiles.shape[0], dtype=jnp.int32) < count_here).astype(jnp.float32)
    picked = slab_image[pixel_rows]
    operand = jnp.stack([picked, jnp.ones_like(picked)], axis=1).astype(jnp.float32)
    products = jnp.einsum('krv,kcv->kcr', block_tiles.astype(jnp.float32), operand)
    products = products * live_mask[:, None, None]
    return jax.ops.segment_sum(products, ray_rows, num_segments=ray_total)


def backward_one(block_tiles, pixel_rows, ray_rows, count_here, ray_values, voxel_total):
    live_mask = (jnp.arange(block_tiles.shape[0], dtype=jnp.int32) < count_here).astype(jnp.float32)
    gathered = ray_values[ray_rows].astype(jnp.float32)
    products = jnp.einsum('krv,kcr->kcv', block_tiles.astype(jnp.float32), gathered)
    products = products * live_mask[:, None, None]
    return jax.ops.segment_sum(products, pixel_rows, num_segments=voxel_total)


def make_ratio(totals, measured, weight, subset):
    ray_rows = jnp.arange(totals.shape[0], dtype=jnp.int32)
    view_of = ray_rows % VG
    in_subset = jnp.any(subset[None, :] == view_of[:, None], axis=1).astype(jnp.float32)
    denominator_rays = weight * totals[:, 1]
    residual_rays = in_subset[:, None] * weight * (measured - totals[:, 0])
    return jnp.stack([denominator_rays, residual_rays], axis=1).astype(jnp.bfloat16)


def reference(volume, tile_blocks, pixel_tile, ray_tile, counts, subset_views, sinogram, weights):
    slab_image = volume.astype(jnp.bfloat16)
    forward_fn = partial(forward_one, ray_total=RT)

    def project_group(operands):
        group_tiles, group_pixels, group_rays, group_counts = operands
        partials = jax.vmap(forward_fn, in_axes=(0, 0, 0, 0, 0))(group_tiles, group_pixels, group_rays, group_counts, slab_image)
        return jnp.sum(partials, axis=0)

    projected = lax.map(project_group, (tile_blocks, pixel_tile, ray_tile, counts))
    back_in = jax.vmap(make_ratio)(projected, sinogram, weights, subset_views)
    backward_fn = partial(backward_one, voxel_total=VT)

    def back_group(operands):
        group_tiles, group_pixels, group_rays, group_counts, group_in = operands
        return jax.vmap(backward_fn, in_axes=(0, 0, 0, 0, None))(group_tiles, group_pixels, group_rays, group_counts, group_in)

    back = jnp.sum(lax.map(back_group, (tile_blocks, pixel_tile, ray_tile, counts, back_in)), axis=0)
    denominators = back[:, :, 0, :]
    gradient = back[:, :, 1, :]
    updated = jnp.maximum(volume + SUBSETS * gradient / denominators, 0.0)
    return updated, denominators
```

```python
import functools

import jax
import jax.numpy as jnp
from jax import lax
from jax.experimental import pallas as pl
from jax.experimental.pallas import tpu as pltpu
from jax.sharding import PartitionSpec as P

VG = 8
SUBSETS = 2
ROWS = 8
UNROLL = 16


def row_of(index):
    return pl.ds(pl.multiple_of(index * ROWS, ROWS), ROWS)


def slot_loop(count, slots, tile_ref, from_ref, to_ref, operand, total, spare, contract):
    def body(step, carry):
        first = step * UNROLL
        for u in range(UNROLL):
            k = first + u
            source = jnp.where(k < count, from_ref[k], spare)
            lhs = operand[row_of(source), :].astype(jnp.bfloat16)
            product = lax.dot_general(
                lhs, tile_ref[k], (((1,), (contract,)), ((), ())),
                preferred_element_type=jnp.float32,
            )
            total[row_of(to_ref[k]), :] += product
        return carry

    lax.fori_loop(0, pl.cdiv(count, UNROLL), body, 0)


def forward_kernel(pixel_ref, ray_ref, count_ref, image_ref, tile_ref, out_ref, operand, total):
    voxel_tiles = image_ref.shape[0]
    ray_tiles = out_ref.shape[1]
    slots = tile_ref.shape[0]
    count = count_ref[0]
    operand[...] = jnp.zeros_like(operand)
    total[...] = jnp.zeros_like(total)
    operand[pl.ds(0, voxel_tiles, stride=ROWS), :] = image_ref[...].astype(jnp.float32)
    operand[pl.ds(1, voxel_tiles, stride=ROWS), :] = jnp.ones(image_ref.shape, jnp.float32)
    slot_loop(count, slots, tile_ref, pixel_ref, ray_ref, operand, total, voxel_tiles, 1)
    for c in range(2):
        out_ref[c] = total[pl.ds(c, ray_tiles, stride=ROWS), :]


def backward_kernel(
    pixel_ref, ray_ref, count_ref, subset_ref, *refs
):
    parts, (sino_ref, weight_ref, tile_ref, out_ref, operand, total) = refs[:-6], refs[-6:]
    ray_tiles = sino_ref.shape[0]
    voxel_tiles = out_ref.shape[1]
    slots = tile_ref.shape[0]
    count = count_ref[0]
    operand[...] = jnp.zeros_like(operand)
    total[...] = jnp.zeros_like(total)
    view_of = lax.broadcasted_iota(jnp.int32, sino_ref.shape, 0) % VG
    listed = view_of == subset_ref[0]
    for j in range(1, subset_ref.shape[0]):
        listed = listed | (view_of == subset_ref[j])
    projected = sum(part[0] for part in parts)
    row_sums = sum(part[1] for part in parts)
    weight = weight_ref[...]
    residual = jnp.where(listed, weight * (sino_ref[...] - projected), 0.0)
    operand[pl.ds(0, ray_tiles, stride=ROWS), :] = weight * row_sums
    operand[pl.ds(1, ray_tiles, stride=ROWS), :] = residual
    slot_loop(count, slots, tile_ref, ray_ref, pixel_ref, operand, total, ray_tiles, 0)
    for c in range(2):
        out_ref[c] = total[pl.ds(c, voxel_tiles, stride=ROWS), :]


def smem():
    return pl.BlockSpec(memory_space=pltpu.SMEM)


def vmem():
    return pl.BlockSpec(memory_space=pltpu.VMEM)


def forward(pixel, ray, count, image, tiles, ray_tiles):
    voxel_tiles, width = image.shape
    return pl.pallas_call(
        forward_kernel,
        out_shape=jax.ShapeDtypeStruct((2, ray_tiles, tiles.shape[1]), jnp.float32),
        in_specs=[smem(), smem(), smem(), vmem(), vmem()],
        out_specs=vmem(),
        scratch_shapes=[
            pltpu.VMEM(((voxel_tiles + 1) * ROWS, width), jnp.float32),
            pltpu.VMEM((ray_tiles * ROWS, tiles.shape[1]), jnp.float32),
        ],
        name="forward",
    )(pixel, ray, count, image, tiles)


def backward(pixel, ray, count, subset, parts, sino, weight, tiles, voxel_tiles):
    ray_tiles, width = sino.shape
    return pl.pallas_call(
        backward_kernel,
        out_shape=jax.ShapeDtypeStruct((2, voxel_tiles, tiles.shape[2]), jnp.float32),
        in_specs=[smem()] * 4 + [vmem()] * (len(parts) + 3),
        out_specs=vmem(),
        scratch_shapes=[
            pltpu.VMEM(((ray_tiles + 1) * ROWS, width), jnp.float32),
            pltpu.VMEM((voxel_tiles * ROWS, tiles.shape[2]), jnp.float32),
        ],
        name="backward",
    )(pixel, ray, count, subset, *parts, sino, weight, tiles)


def swap(x, axis, bit):
    return lax.ppermute(x, axis, [(i, i ^ bit) for i in range(lax.axis_size(axis))])


def bits(axis):
    return [1 << b for b in range(lax.axis_size(axis).bit_length() - 1)]


def gather_xor(x, axis):
    x = x[None]
    for bit in bits(axis):
        x = jnp.concatenate([x, swap(x, axis, bit)], axis=0)
    return x


def gather(x, axis):
    me = lax.axis_index(axis)
    blocks = gather_xor(x, axis)
    return blocks[jnp.arange(blocks.shape[0]) ^ me].reshape((-1,) + x.shape[1:])


def on_device(volume, tile_blocks, pixel_tile, ray_tile, counts, subset_views, sinogram, weights):
    tiles, pixel, ray, count = tile_blocks[0, 0], pixel_tile[0, 0], ray_tile[0, 0], counts[0]
    views = lax.axis_size("view")
    ray_total = sinogram.shape[1] * lax.axis_size("slab")
    voxel_total = volume.shape[1] * views
    image = gather(volume[0].astype(jnp.bfloat16), "view")
    measured = gather(jnp.stack([sinogram[0], weights[0]], axis=1), "slab")
    partial = forward(pixel, ray, count, image, tiles, ray_total)
    for bit in reversed(bits("slab")):
        partial = partial + swap(partial, "slab", bit)
    back = backward(
        pixel, ray, count, subset_views[0], [partial],
        measured[:, 0], measured[:, 1], tiles, voxel_total,
    )
    me = lax.axis_index("view")
    blocks = back.reshape(2, views, volume.shape[1], volume.shape[2])
    blocks = blocks[:, jnp.arange(views) ^ me].swapaxes(0, 1)
    for bit in bits("view"):
        rest = blocks.reshape((-1, 2) + blocks.shape[1:])
        blocks = rest[:, 0] + swap(rest[:, 1], "view", bit)
    denominators, gradient = blocks[0, 0], blocks[0, 1]
    updated = jnp.maximum(volume[0] + SUBSETS * gradient / denominators, 0.0)
    return (updated[None], denominators[None])


def solution(mesh):
    return jax.shard_map(
        on_device,
        mesh=mesh,
        in_specs=(
            P("slab", "view", None),
            P("view", "slab", None, None, None),
            P("view", "slab", None),
            P("view", "slab", None),
            P("view", "slab"),
            P("view", None),
            P("view", "slab", None),
            P("view", "slab", None),
        ),
        out_specs=(P("slab", "view", None), P("slab", "view", None)),
        check_vma=False,
    )
```

```python
import jax
import jax.numpy as jnp
from jax import lax
from jax.experimental import pallas as pl
from jax.experimental.pallas import tpu as pltpu
from jax.sharding import PartitionSpec as P

VG = 8
SUBSETS = 2
ROWS = 8
UNROLL = 64
LOADS = 8


def row_of(index):
    return pl.ds(pl.multiple_of(index * ROWS, ROWS), ROWS)


def relative(tile, size, me):
    if size & (size - 1) == 0:
        return tile ^ (me * size)
    return (lax.div(tile, size) ^ me) * size + lax.rem(tile, size)


def fill(operand, first, tiles, stride, columns):
    for c, column in enumerate(columns):
        for at in (c, c + 2):
            operand[pl.ds(first + at, tiles, stride=stride), :] = column


def slot_loop(count, tile_ref, source_of, target_of, operand, total, spare, forward):
    width = operand.shape[1]
    row = lax.broadcasted_iota(jnp.int32, (ROWS, width), 0)
    rows = row < 2, (row >= 2) & (row < 4)

    def body(step, carry):
        first = step * UNROLL
        for u in range(0, UNROLL, 2):
            pair = first + u, first + u + 1
            lhs = []
            for k, mine in zip(pair, rows):
                source = jnp.where(k < count, source_of(k), spare)
                lhs.append(jnp.where(mine, operand[row_of(source), :], 0.0))
            lhs = jnp.concatenate(lhs, axis=1) if forward else lhs[0] + lhs[1]
            product = lax.dot_general(
                lhs.astype(jnp.bfloat16),
                jnp.concatenate([tile_ref[k] for k in pair], axis=1),
                (((1,), (1 if forward else 0,)), ((), ())),
                preferred_element_type=jnp.float32,
            )
            for i, (k, mine) in enumerate(zip(pair, rows)):
                part = product if forward else product[:, i * width : (i + 1) * width]
                total[row_of(target_of(k)), :] += jnp.where(mine, part, 0.0)
        return carry

    lax.fori_loop(0, pl.cdiv(count, UNROLL), body, 0)


def summed(total, first, tiles, stride):
    return total[pl.ds(first, tiles, stride=stride), :] + total[pl.ds(first + 2, tiles, stride=stride), :]


def load_kernel(*refs):
    half = (len(refs) - 1) // 2
    pairs = list(zip(refs[:half], refs[half:-1]))
    tiles, tiles_out = pairs.pop()
    chunk = -(-tiles.shape[0] // LOADS)
    for at in range(0, tiles.shape[0], chunk):
        rows = pl.ds(at, min(chunk, tiles.shape[0] - at))
        pairs.append((tiles.at[rows], tiles_out.at[rows]))
    copies = [
        pltpu.make_async_copy(src, dst, refs[-1].at[i]) for i, (src, dst) in enumerate(pairs)
    ]
    for copy in copies:
        copy.start()
    for copy in copies:
        copy.wait()


def forward_kernel(
    pixel_ref, ray_ref, count_ref, subset_ref, image_ref, sino_ref, weight_ref, tile_ref,
    out_ref, operand, total,
):
    me = lax.axis_index("view")
    views, size, width = image_ref.shape
    voxel_tiles = views * size
    ray_tiles = total.shape[0] // ROWS - VG
    total[...] = jnp.zeros_like(total)
    operand[row_of(voxel_tiles), :] = jnp.zeros((ROWS, width), jnp.float32)
    image = image_ref[...].astype(jnp.float32).reshape(voxel_tiles, width)
    fill(operand, 0, voxel_tiles, ROWS, (image, jnp.ones_like(image)))
    slot_loop(
        count_ref[0, 0], tile_ref, lambda k: relative(pixel_ref[k], size, me),
        lambda k: ray_ref[k], operand, total, voxel_tiles, True,
    )
    out_ref[pl.ds(0, ray_tiles), :] = summed(total, 1, ray_tiles, ROWS)
    turns = ray_tiles // VG
    at = ray_tiles
    for j in range(subset_ref.shape[0]):
        first = pl.multiple_of(subset_ref[j] * ROWS, ROWS)
        out_ref[pl.ds(at, turns), :] = summed(total, first, turns, ROWS * VG)
        at += turns
    own = sino_ref.shape[0]
    out_ref[pl.ds(at, own), :] = sino_ref[...]
    out_ref[pl.ds(at + own, own), :] = weight_ref[...]


def backward_kernel(pixel_ref, ray_ref, count_ref, subset_ref, *refs):
    parts, (tile_ref, keep_ref, send_ref, operand, total, sino, weight) = refs[:-7], refs[-7:]
    me, slab = lax.axis_index("view"), lax.axis_index("slab")
    ray_tiles, width = sino.shape[0] - VG, sino.shape[1]
    half, _, size, _ = keep_ref.shape
    own = ray_tiles // len(parts)
    turns = ray_tiles // VG
    subset = subset_ref.shape[0]
    measured = ray_tiles + subset * turns
    total[...] = jnp.zeros_like(total)
    operand[row_of(ray_tiles), :] = jnp.zeros((ROWS, width), jnp.float32)
    for j, part in enumerate(parts):
        first = pl.multiple_of((slab ^ j) * own, own)
        sino[pl.ds(first, own), :] = part[pl.ds(measured, own), :]
        weight[pl.ds(first, own), :] = part[pl.ds(measured + own, own), :]
    row_sums = sum(part[pl.ds(0, ray_tiles), :] for part in parts)
    column = weight[pl.ds(0, ray_tiles), :] * row_sums
    fill(operand, 0, ray_tiles, ROWS, (column, jnp.zeros_like(column)))
    for j in range(subset):
        view = subset_ref[j]
        projected = sum(part[pl.ds(ray_tiles + j * turns, turns), :] for part in parts)
        rows = pl.ds(view, turns, stride=VG)
        residual = weight[rows, :] * (sino[rows, :] - projected)
        for at in (1, 3):
            operand[pl.ds(view * ROWS + at, turns, stride=ROWS * VG), :] = residual
    slot_loop(
        count_ref[0, 0], tile_ref, lambda k: ray_ref[k],
        lambda k: relative(pixel_ref[k], size, me), operand, total, ray_tiles, False,
    )
    for j in range(2 * half):
        out = send_ref if j % 2 else keep_ref
        for c in range(2):
            out[j // 2, c] = summed(total, j * size * ROWS + c, size, ROWS)


def smem():
    return pl.BlockSpec(memory_space=pltpu.SMEM)


def vmem():
    return pl.BlockSpec(memory_space=pltpu.VMEM)


def in_vmem(x):
    return pltpu.with_memory_space_constraint(x, pltpu.VMEM)


def in_smem(x):
    return pltpu.with_memory_space_constraint(x, pltpu.SMEM)


LIMIT = pltpu.CompilerParams(vmem_limit_bytes=16 << 20)


def load(tables, arrays):
    inputs = (*tables, *arrays)
    return pl.pallas_call(
        load_kernel,
        out_shape=[pltpu.SMEM(x.shape, x.dtype) for x in tables]
        + [pltpu.VMEM(x.shape, x.dtype) for x in arrays],
        in_specs=[pl.BlockSpec(memory_space=pl.ANY if x.size == 1 else pltpu.HBM) for x in inputs],
        out_specs=[smem()] * len(tables) + [vmem()] * len(arrays),
        scratch_shapes=[pltpu.SemaphoreType.DMA((len(tables) + len(arrays) + LOADS,))],
        compiler_params=LIMIT,
        cost_estimate=pl.CostEstimate(flops=0, transcendentals=0, bytes_accessed=32 << 20),
        name="load",
    )(*(x if x.size == 1 else pltpu.with_memory_space_constraint(x, pltpu.HBM) for x in inputs))


def forward(pixel, ray, count, subset, image, sino, weight, tiles, ray_tiles):
    width = image.shape[2]
    voxel_tiles = image.shape[0] * image.shape[1]
    rows = ray_tiles + subset.shape[0] * (ray_tiles // VG) + 2 * sino.shape[0]
    return pl.pallas_call(
        forward_kernel,
        out_shape=jax.ShapeDtypeStruct((rows, tiles.shape[1]), jnp.float32),
        in_specs=[smem()] * 4 + [vmem()] * 4,
        out_specs=vmem(),
        scratch_shapes=[
            pltpu.VMEM(((voxel_tiles + 1) * ROWS, width), jnp.float32),
            pltpu.VMEM(((ray_tiles + VG) * ROWS, tiles.shape[1]), jnp.float32),
        ],
        compiler_params=LIMIT,
        name="forward",
    )(*map(in_smem, (pixel, ray, count, subset)), image, in_vmem(sino), in_vmem(weight), in_vmem(tiles))


def backward(pixel, ray, count, subset, parts, tiles, ray_tiles, views, size):
    width = tiles.shape[1]
    half = jax.ShapeDtypeStruct((views // 2, 2, size, tiles.shape[2]), jnp.float32)
    return pl.pallas_call(
        backward_kernel,
        out_shape=(half, half),
        in_specs=[smem()] * 4 + [vmem()] * (len(parts) + 1),
        out_specs=(vmem(), vmem()),
        scratch_shapes=[
            pltpu.VMEM(((ray_tiles + VG) * ROWS, width), jnp.float32),
            pltpu.VMEM(((views * size + 1) * ROWS, tiles.shape[2]), jnp.float32),
            pltpu.VMEM((ray_tiles + VG, width), jnp.float32),
            pltpu.VMEM((ray_tiles + VG, width), jnp.float32),
        ],
        compiler_params=LIMIT,
        name="backward",
    )(*map(in_smem, (pixel, ray, count, subset)), *parts, in_vmem(tiles))


def swap(x, axis, bit):
    return lax.ppermute(x, axis, [(i, i ^ bit) for i in range(lax.axis_size(axis))])


def bits(axis):
    return [1 << b for b in range(lax.axis_size(axis).bit_length() - 1)]


def on_device(volume, tile_blocks, pixel_tile, ray_tile, counts, subset_views, sinogram, weights):
    tiles, pixel, ray = tile_blocks[0, 0], pixel_tile[0, 0], ray_tile[0, 0]
    views, slabs = lax.axis_size("view"), lax.axis_size("slab")
    ray_tiles = sinogram.shape[1] * slabs
    pixel, ray, count, subset, sino, weight, tiles = load(
        (pixel, ray, counts, subset_views[0]), (sinogram[0], weights[0], tiles)
    )
    image = volume
    for bit in bits("view"):
        image = jnp.concatenate([image, swap(image, "view", bit)], axis=0).astype(jnp.bfloat16)
    own = forward(
        pixel, ray, count, subset, image, sino, weight, tiles, ray_tiles
    )
    parts = {0: own}
    for bit in reversed(bits("slab")):
        parts |= {j | bit: swap(part, "slab", bit) for j, part in parts.items()}
    parts = [parts[j] for j in range(slabs)]
    keep, send = backward(
        pixel, ray, count, subset, parts, tiles, ray_tiles, views, volume.shape[1]
    )
    for bit in bits("view"):
        blocks = keep + swap(send, "view", bit)
        keep, send = blocks[::2], blocks[1::2]
    denominators, gradient = keep[0, 0], keep[0, 1]
    updated = jnp.maximum(volume[0] + SUBSETS * gradient / denominators, 0.0)
    return (updated[None], denominators[None])


def solution(mesh):
    return jax.shard_map(
        on_device,
        mesh=mesh,
        in_specs=(
            P("slab", "view", None),
            P("view", "slab", None, None, None),
            P("view", "slab", None),
            P("view", "slab", None),
            P("view", "slab"),
            P("view", None),
            P("view", "slab", None),
            P("view", "slab", None),
        ),
        out_specs=(P("slab", "view", None), P("slab", "view", None)),
        check_vma=False,
    )
```

```python
import jax
import jax.numpy as jnp
from jax import lax
from jax.experimental import pallas as pl
from jax.experimental.pallas import tpu as pltpu
from jax.sharding import PartitionSpec as P

VG = 8
SUBSETS = 2
ROWS = 8
BLOCKS = 64, 16
LOADS = 8
FIELD = 10


def row_of(index):
    return pl.ds(pl.multiple_of(index * ROWS, ROWS), ROWS)


def relative(tile, size, me):
    if size & (size - 1) == 0:
        return tile ^ (me * size)
    return (lax.div(tile, size) ^ me) * size + lax.rem(tile, size)


def fill(operand, first, tiles, stride, columns):
    for c, column in enumerate(columns):
        for at in (c, c + 2):
            operand[pl.ds(first + at, tiles, stride=stride), :] = column


def packed(slot, ray, place):
    return slot | (ray << FIELD) | (place << (2 * FIELD))


def unpacked(word):
    mask = (1 << FIELD) - 1
    return word & mask, (word >> FIELD) & mask, word >> (2 * FIELD)


def make_lists(slots, count, pixel_ref, ray_ref, list_refs, length_ref, choose, place_of, pad):
    def body(step, ends):
        for u in range(8):
            k = step * 8 + u
            place = place_of(pixel_ref[k])
            word = packed(k, ray_ref[k], place)
            live = (k < count).astype(jnp.int32)
            second = choose(place)
            for ref, end in zip(list_refs, ends):
                ref[end] = word
            ends = ends[0] + live * (1 - second), ends[1] + live * second
        return ends

    ends = lax.fori_loop(0, slots // 8, body, (jnp.int32(0), jnp.int32(0)))
    for i, (ref, end) in enumerate(zip(list_refs, ends)):
        length_ref[i] = end

        def pad_body(j, carry, ref=ref, end=end):
            ref[end + j] = pad
            return carry

        lax.fori_loop(0, BLOCKS[-1], pad_body, 0, unroll=True)


def slot_loop(list_ref, length, tile_ref, operand, total, forward):
    width = operand.shape[1]
    row = lax.broadcasted_iota(jnp.int32, (ROWS, width), 0)
    rows = row < 2, (row >= 2) & (row < 4)

    def block(first, size):
        for u in range(0, size, 2):
            pair = [unpacked(list_ref[first + u + i]) for i in range(2)]
            lhs = [
                jnp.where(mine, operand[row_of(place if forward else ray), :], 0.0)
                for (_, ray, place), mine in zip(pair, rows)
            ]
            lhs = jnp.concatenate(lhs, axis=1) if forward else lhs[0] + lhs[1]
            product = lax.dot_general(
                lhs.astype(jnp.bfloat16),
                jnp.concatenate([tile_ref[slot] for slot, _, _ in pair], axis=1),
                (((1,), (1 if forward else 0,)), ((), ())),
                preferred_element_type=jnp.float32,
            )
            for i, ((_, ray, place), mine) in enumerate(zip(pair, rows)):
                part = product if forward else product[:, i * width : (i + 1) * width]
                total[row_of(ray if forward else place), :] += jnp.where(mine, part, 0.0)

    done = jnp.int32(0)
    for size in BLOCKS:
        steps = lax.div(length - done + (size - 1 if size == BLOCKS[-1] else 0), size)

        def body(step, carry, done=done, size=size):
            block(done + step * size, size)
            return carry

        lax.fori_loop(0, steps, body, 0)
        done += steps * size


def summed(total, first, tiles, stride):
    return total[pl.ds(first, tiles, stride=stride), :] + total[pl.ds(first + 2, tiles, stride=stride), :]


def copy_all(pairs, sems):
    copies = [pltpu.make_async_copy(src, dst, sems.at[i]) for i, (src, dst) in enumerate(pairs)]
    for copy in copies:
        copy.start()
    return copies


def first_kernel(*refs):
    half = (len(refs) - 2) // 2
    inputs, outputs, (volume_ref, sems) = refs[:half], refs[half:-2], refs[-2:]
    *outputs, own_ref = outputs
    for copy in copy_all(list(zip(inputs, [*outputs, volume_ref])), sems):
        copy.wait()
    own_ref[...] = volume_ref[...].astype(jnp.bfloat16)


def tile_copies(tiles_in, tiles_ref, sems, part):
    half = -(-tiles_in.shape[0] // 2)
    first, last = (0, half) if part == 0 else (half, tiles_in.shape[0])
    chunk = -(-(last - first) // LOADS)
    rows = [pl.ds(at, min(chunk, last - at)) for at in range(first, last, chunk)]
    return copy_all([(tiles_in.at[r], tiles_ref.at[r]) for r in rows], sems)


def lists_kernel(
    own_ref, count_ref, pixel_ref, ray_ref, tiles_in,
    early_ref, late_ref, length_ref, image_ref, tiles_ref, sems, *, size, views, ray_tiles,
):
    me = lax.axis_index("view")
    copies = tile_copies(tiles_in, tiles_ref, sems, 0)
    image_ref[0] = own_ref[...]
    half = views * size // 2
    make_lists(
        pixel_ref.shape[0], count_ref[0, 0], pixel_ref, ray_ref, (early_ref, late_ref), length_ref,
        lambda place: (place >= half).astype(jnp.int32), lambda tile: relative(tile, size, me),
        packed(0, ray_tiles, views * size),
    )
    for copy in copies:
        copy.wait()


def tiles_kernel(image_in, tiles_in, _, image_ref, tiles_ref, sems):
    copies = tile_copies(tiles_in, tiles_ref, sems, 1)
    image_ref[...] = image_in[...]
    for copy in copies:
        copy.wait()


def clear(ref, tiles):
    ref[row_of(tiles), :] = jnp.zeros((ROWS, ref.shape[1]), jnp.float32)


def early_kernel(list_ref, length_ref, image_ref, tile_ref, total, operand):
    blocks, size, width = image_ref.shape
    tiles = blocks * size
    total[...] = jnp.zeros_like(total)
    clear(operand, 2 * tiles)
    image = image_ref[...].astype(jnp.float32).reshape(tiles, width)
    fill(operand, 0, tiles, ROWS, (image, jnp.ones_like(image)))
    slot_loop(list_ref, length_ref[0], tile_ref, operand, total, True)


def late_kernel(
    list_ref, length_ref, subset_ref, image_ref, sino_ref, weight_ref, tile_ref, total_in,
    out_ref, total, operand,
):
    blocks, size, width = image_ref.shape
    tiles = blocks * size
    ray_tiles = total.shape[0] // ROWS - VG
    clear(operand, 2 * tiles)
    image = image_ref[...].astype(jnp.float32).reshape(tiles, width)
    fill(operand, tiles * ROWS, tiles, ROWS, (image, jnp.ones_like(image)))
    slot_loop(list_ref, length_ref[1], tile_ref, operand, total, True)
    out_ref[pl.ds(0, ray_tiles), :] = summed(total, 1, ray_tiles, ROWS)
    turns = ray_tiles // VG
    at = ray_tiles
    for j in range(subset_ref.shape[0]):
        first = pl.multiple_of(subset_ref[j] * ROWS, ROWS)
        out_ref[pl.ds(at, turns), :] = summed(total, first, turns, ROWS * VG)
        at += turns
    own = sino_ref.shape[0]
    out_ref[pl.ds(at, own), :] = sino_ref[...]
    out_ref[pl.ds(at + own, own), :] = weight_ref[...]


def split_kernel(pixel_ref, ray_ref, count_ref, after_ref, keep_ref, send_ref, length_ref, *, size, views, ray_tiles):
    me = lax.axis_index("view")
    make_lists(
        pixel_ref.shape[0], count_ref[0, 0], pixel_ref, ray_ref, (keep_ref, send_ref), length_ref,
        lambda place: lax.div(place, size) & 1, lambda tile: relative(tile, size, me),
        packed(0, ray_tiles, views * size),
    )


def send_kernel(list_ref, length_ref, subset_ref, *refs):
    parts, (tile_ref, out_ref, operand, total, sino, weight) = refs[:-6], refs[-6:]
    slab = lax.axis_index("slab")
    ray_tiles, width = sino.shape[0] - VG, sino.shape[1]
    own = ray_tiles // len(parts)
    turns = ray_tiles // VG
    subset = subset_ref.shape[0]
    measured = ray_tiles + subset * turns
    total[...] = jnp.zeros_like(total)
    clear(operand, ray_tiles)
    for j, part in enumerate(parts):
        first = pl.multiple_of((slab ^ j) * own, own)
        sino[pl.ds(first, own), :] = part[pl.ds(measured, own), :]
        weight[pl.ds(first, own), :] = part[pl.ds(measured + own, own), :]
    row_sums = sum(part[pl.ds(0, ray_tiles), :] for part in parts)
    column = weight[pl.ds(0, ray_tiles), :] * row_sums
    fill(operand, 0, ray_tiles, ROWS, (column, jnp.zeros_like(column)))
    for j in range(subset):
        view = subset_ref[j]
        projected = sum(part[pl.ds(ray_tiles + j * turns, turns), :] for part in parts)
        rows = pl.ds(view, turns, stride=VG)
        residual = weight[rows, :] * (sino[rows, :] - projected)
        for at in (1, 3):
            operand[pl.ds(view * ROWS + at, turns, stride=ROWS * VG), :] = residual
    slot_loop(list_ref, length_ref[1], tile_ref, operand, total, False)
    write_blocks(total, out_ref, 1)


def keep_kernel(list_ref, length_ref, operand, tile_ref, out_ref, total):
    total[...] = jnp.zeros_like(total)
    slot_loop(list_ref, length_ref[0], tile_ref, operand, total, False)
    write_blocks(total, out_ref, 0)


def write_blocks(total, out_ref, odd):
    half, _, size, _ = out_ref.shape
    for j in range(half):
        for c in range(2):
            out_ref[j, c] = summed(total, (2 * j + odd) * size * ROWS + c, size, ROWS)


SMEM, VMEM, HBM = (pl.BlockSpec(memory_space=m) for m in (pltpu.SMEM, pltpu.VMEM, pltpu.HBM))
LIMIT = pltpu.CompilerParams(vmem_limit_bytes=16 << 20)


def call(kernel, name, inputs, outputs, scratch=(), aliases=None, cost=0):
    spaces = {pltpu.SMEM: SMEM, pltpu.VMEM: VMEM, pltpu.HBM: HBM}
    keys = [pltpu.SMEM if x.memory_space == pltpu.SMEM else pltpu.VMEM for x in outputs]
    return pl.pallas_call(
        kernel,
        out_shape=outputs,
        in_specs=[SMEM if m is None else spaces[m] for _, m in inputs],
        out_specs=[spaces[m] for m in keys],
        scratch_shapes=list(scratch),
        compiler_params=LIMIT,
        input_output_aliases=aliases or {},
        cost_estimate=pl.CostEstimate(flops=0, transcendentals=0, bytes_accessed=cost),
        name=name,
    )(*(x if m is None else pltpu.with_memory_space_constraint(x, m) for x, m in inputs))


def swap(x, axis, bit):
    return lax.ppermute(x, axis, [(i, i ^ bit) for i in range(lax.axis_size(axis))])


def bits(axis):
    return [1 << b for b in range(lax.axis_size(axis).bit_length() - 1)]


def on_device(volume, tile_blocks, pixel_tile, ray_tile, counts, subset_views, sinogram, weights):
    views, slabs = lax.axis_size("view"), lax.axis_size("slab")
    _, size, width = volume.shape
    slots, depth = tile_blocks.shape[2], tile_blocks.shape[3]
    own_rays = sinogram.shape[1]
    ray_tiles, voxel_tiles = own_rays * slabs, size * views
    turns = ray_tiles // VG
    sizes = dict(size=size, views=views, ray_tiles=ray_tiles)
    words = pltpu.SMEM((slots + BLOCKS[-1],), jnp.int32)
    lengths = pltpu.SMEM((2,), jnp.int32)
    measured = pltpu.VMEM((own_rays, depth), jnp.float32)
    hbm = pltpu.HBM

    smem, vmem = pltpu.SMEM, pltpu.VMEM
    table = pltpu.SMEM((slots,), jnp.int32)
    on_chip = pltpu.VMEM((slots, depth, width), jnp.bfloat16)
    pixel, ray, subset, sino, weight, own = call(
        first_kernel, "first",
        [(pixel_tile[0, 0], hbm), (ray_tile[0, 0], hbm), (subset_views[0], hbm),
         (sinogram[0], hbm), (weights[0], hbm), (volume[0], hbm)],
        [table, table, pltpu.SMEM((subset_views.shape[1],), jnp.int32), measured, measured,
         pltpu.VMEM((size, width), jnp.bfloat16)],
        [pltpu.VMEM((size, width), jnp.float32), pltpu.SemaphoreType.DMA((6,))],
    )
    view_bits = bits("view")
    arrived = swap(own[None], "view", view_bits[0])
    early, late, forward_lengths, image, tiles = call(
        lambda *refs: lists_kernel(*refs, **sizes), "lists",
        [(own, vmem), (counts, None), (pixel, smem), (ray, smem), (tile_blocks[0, 0], hbm)],
        [words, words, lengths, pltpu.VMEM((1, size, width), jnp.bfloat16), on_chip],
        [pltpu.SemaphoreType.DMA((LOADS,))], cost=8 << 20,
    )
    for bit in view_bits[1:]:
        image = jnp.concatenate([image, arrived], axis=0)
        arrived = swap(image, "view", bit)
        if bit == view_bits[1]:
            image, tiles = call(
                tiles_kernel, "tiles",
                [(image, vmem), (tile_blocks[0, 0], hbm), (tiles, vmem)],
                [pltpu.VMEM(image.shape, image.dtype), on_chip],
                [pltpu.SemaphoreType.DMA((LOADS,))], aliases={2: 1}, cost=8 << 20,
            )
    sums = pltpu.VMEM(((ray_tiles + VG) * ROWS, depth), jnp.float32)
    image_operand = pltpu.VMEM(((voxel_tiles + 1) * ROWS, width), jnp.float32)
    (total,) = call(
        early_kernel, "early",
        [(early, smem), (forward_lengths, smem), (image, vmem), (tiles, vmem)],
        [sums], [image_operand], cost=8 << 20,
    )
    rows = ray_tiles + subset_views.shape[1] * turns + 2 * own_rays
    part, _ = call(
        late_kernel, "late",
        [(late, smem), (forward_lengths, smem), (subset, smem), (arrived, vmem), (sino, vmem),
         (weight, vmem), (tiles, vmem), (total, vmem)],
        [pltpu.VMEM((rows, depth), jnp.float32), sums], [image_operand], aliases={7: 1},
    )
    parts = {0: part}
    for bit in reversed(bits("slab")):
        parts |= {j | bit: swap(p, "slab", bit) for j, p in parts.items()}
    keep_list, send_list, back_lengths = call(
        lambda *refs: split_kernel(*refs, **sizes), "split",
        [(pixel, smem), (ray, smem), (counts, None), (part, vmem)], [words, words, lengths],
        cost=4 << 20,
    )
    blocks = pltpu.VMEM((views // 2, 2, size, width), jnp.float32)
    back_sums = pltpu.VMEM(((voxel_tiles + 1) * ROWS, width), jnp.float32)
    rays = pltpu.VMEM((ray_tiles + VG, depth), jnp.float32)
    send, operand = call(
        send_kernel, "send",
        [(send_list, smem), (back_lengths, smem), (subset, smem)]
        + [(parts[j], vmem) for j in range(slabs)] + [(tiles, vmem)],
        [blocks, sums], [back_sums, rays, rays],
    )
    (keep,) = call(
        keep_kernel, "keep",
        [(keep_list, smem), (back_lengths, smem), (operand, vmem), (tiles, vmem)],
        [blocks], [back_sums], cost=8 << 20,
    )
    for bit in view_bits:
        both = keep + swap(send, "view", bit)
        keep, send = both[::2], both[1::2]
    denominators, gradient = keep[0, 0], keep[0, 1]
    updated = jnp.maximum(volume[0] + SUBSETS * gradient / denominators, 0.0)
    return (updated[None], denominators[None])


def solution(mesh):
    return jax.shard_map(
        on_device,
        mesh=mesh,
        in_specs=(
            P("slab", "view", None),
            P("view", "slab", None, None, None),
            P("view", "slab", None),
            P("view", "slab", None),
            P("view", "slab"),
            P("view", None),
            P("view", "slab", None),
            P("view", "slab", None),
        ),
        out_specs=(P("slab", "view", None), P("slab", "view", None)),
        check_vma=False,
    )
```

```python
import jax
import jax.numpy as jnp
from jax import lax
from jax.experimental import pallas as pl
from jax.experimental.pallas import tpu as pltpu
from jax.sharding import PartitionSpec as P

VG = 8
SUBSETS = 2
ROWS = 8
BLOCKS = 64, 16
LOADS = 8
EARLY_TILES = 45
FIELD = 10


def row_of(index):
    return pl.ds(pl.multiple_of(index * ROWS, ROWS), ROWS)


def relative(tile, size, me):
    if size & (size - 1) == 0:
        return tile ^ (me * size)
    return (lax.div(tile, size) ^ me) * size + lax.rem(tile, size)


def fill(operand, first, tiles, stride, columns):
    for c, column in enumerate(columns):
        for at in (c, c + 2):
            operand[pl.ds(first + at, tiles, stride=stride), :] = column


def packed(slot, ray, place):
    return slot | (ray << FIELD) | (place << (2 * FIELD))


def unpacked(word):
    mask = (1 << FIELD) - 1
    return word & mask, (word >> FIELD) & mask, word >> (2 * FIELD)


def make_lists(slots, pixel_ref, ray_ref, list_refs, ends_ref, choose, place_of):
    def body(step, ends):
        for u in range(8):
            k = step * 8 + u
            place = place_of(pixel_ref[k])
            word = packed(k, ray_ref[k], place)
            second = choose(place)
            ends_ref[k] = ends[1]
            for ref, end in zip(list_refs, ends):
                ref[end] = word
            ends = ends[0] + (1 - second), ends[1] + second
        return ends

    ends = lax.fori_loop(0, slots // 8, body, (jnp.int32(0), jnp.int32(0)))
    ends_ref[slots] = ends[1]


def lengths(count_ref, ends_ref):
    count = count_ref[0, 0]
    second = ends_ref[count]
    return count - second, second


def slot_loop(list_ref, length, pad, tile_ref, operand, total, forward):
    width = operand.shape[1]
    row = lax.broadcasted_iota(jnp.int32, (ROWS, width), 0)
    rows = row < 2, (row >= 2) & (row < 4)

    def block(first, size):
        for u in range(0, size, 2):
            pair = [list_ref[first + u + i] for i in range(2)]
            if size == BLOCKS[-1]:
                pair = [jnp.where(first + u + i < length, w, pad) for i, w in enumerate(pair)]
            pair = [unpacked(word) for word in pair]
            lhs = [
                jnp.where(mine, operand[row_of(place if forward else ray), :], 0.0)
                for (_, ray, place), mine in zip(pair, rows)
            ]
            lhs = jnp.concatenate(lhs, axis=1) if forward else lhs[0] + lhs[1]
            product = lax.dot_general(
                lhs.astype(jnp.bfloat16),
                jnp.concatenate([tile_ref[slot] for slot, _, _ in pair], axis=1),
                (((1,), (1 if forward else 0,)), ((), ())),
                preferred_element_type=jnp.float32,
            )
            for i, ((_, ray, place), mine) in enumerate(zip(pair, rows)):
                part = product if forward else product[:, i * width : (i + 1) * width]
                total[row_of(ray if forward else place), :] += jnp.where(mine, part, 0.0)

    done = jnp.int32(0)
    for size in BLOCKS:
        steps = lax.div(length - done + (size - 1 if size == BLOCKS[-1] else 0), size)

        def body(step, carry, done=done, size=size):
            block(done + step * size, size)
            return carry

        lax.fori_loop(0, steps, body, 0)
        done += steps * size


def summed(total, first, tiles, stride):
    return total[pl.ds(first, tiles, stride=stride), :] + total[pl.ds(first + 2, tiles, stride=stride), :]


def copy_all(pairs, sems):
    copies = [pltpu.make_async_copy(src, dst, sems.at[i]) for i, (src, dst) in enumerate(pairs)]
    for copy in copies:
        copy.start()
    return copies


def tile_copies(tiles_in, tiles_ref, sems, part):
    cut = tiles_in.shape[0] * EARLY_TILES // 100
    first, last = (0, cut) if part == 0 else (cut, tiles_in.shape[0])
    chunk = -(-(last - first) // LOADS)
    rows = [pl.ds(at, min(chunk, last - at)) for at in range(first, last, chunk)]
    return copy_all([(tiles_in.at[r], tiles_ref.at[r]) for r in rows], sems)


def first_kernel(*refs):
    half = (len(refs) - 2) // 2
    (*inputs, tiles_in), (*outputs, tiles_ref), (sems, tile_sems) = refs[:half], refs[half:-2], refs[-2:]
    copies = copy_all(list(zip(inputs, outputs)), sems)
    copies += tile_copies(tiles_in, tiles_ref, tile_sems, 0)
    for copy in copies:
        copy.wait()


def lists_kernel(
    image_in, pixel_ref, ray_ref, tiles_in, _, early_ref, late_ref, ends_ref, image_ref, tiles_ref, sems,
    *, size, views,
):
    me = lax.axis_index("view")
    copies = tile_copies(tiles_in, tiles_ref, sems, 1)
    image_ref[...] = image_in[...]
    half = views * size // 2
    make_lists(
        pixel_ref.shape[0], pixel_ref, ray_ref, (early_ref, late_ref), ends_ref,
        lambda place: (place >= half).astype(jnp.int32), lambda tile: relative(tile, size, me),
    )
    for copy in copies:
        copy.wait()


def clear(ref, tiles):
    ref[row_of(tiles), :] = jnp.zeros((ROWS, ref.shape[1]), jnp.float32)


def rounded(image_ref):
    image = image_ref[...].astype(jnp.bfloat16).astype(jnp.float32)
    return image.reshape(-1, image.shape[-1])


def early_kernel(list_ref, ends_ref, count_ref, image_ref, tile_ref, total, operand):
    image = rounded(image_ref)
    tiles = image.shape[0]
    total[...] = jnp.zeros_like(total)
    clear(operand, 2 * tiles)
    fill(operand, 0, tiles, ROWS, (image, jnp.ones_like(image)))
    pad = packed(0, total.shape[0] // ROWS - VG, 2 * tiles)
    slot_loop(list_ref, lengths(count_ref, ends_ref)[0], pad, tile_ref, operand, total, True)


def late_kernel(
    list_ref, ends_ref, count_ref, subset_ref, image_ref, sino_ref, weight_ref, tile_ref, total_in,
    out_ref, total, operand,
):
    image = rounded(image_ref)
    tiles = image.shape[0]
    ray_tiles = total.shape[0] // ROWS - VG
    clear(operand, 2 * tiles)
    fill(operand, tiles * ROWS, tiles, ROWS, (image, jnp.ones_like(image)))
    pad = packed(0, ray_tiles, 2 * tiles)
    slot_loop(list_ref, lengths(count_ref, ends_ref)[1], pad, tile_ref, operand, total, True)
    out_ref[pl.ds(0, ray_tiles), :] = summed(total, 1, ray_tiles, ROWS)
    turns = ray_tiles // VG
    at = ray_tiles
    for j in range(subset_ref.shape[0]):
        first = pl.multiple_of(subset_ref[j] * ROWS, ROWS)
        out_ref[pl.ds(at, turns), :] = summed(total, first, turns, ROWS * VG)
        at += turns
    own = sino_ref.shape[0]
    out_ref[pl.ds(at, own), :] = sino_ref[...]
    out_ref[pl.ds(at + own, own), :] = weight_ref[...]


def split_kernel(pixel_ref, ray_ref, after_ref, keep_ref, send_ref, ends_ref, *, size, views):
    me = lax.axis_index("view")
    make_lists(
        pixel_ref.shape[0], pixel_ref, ray_ref, (keep_ref, send_ref), ends_ref,
        lambda place: lax.div(place, size) & 1, lambda tile: relative(tile, size, me),
    )


def send_kernel(list_ref, ends_ref, count_ref, subset_ref, *refs):
    parts, (tile_ref, out_ref, operand, total, sino, weight) = refs[:-6], refs[-6:]
    slab = lax.axis_index("slab")
    ray_tiles, width = sino.shape[0] - VG, sino.shape[1]
    own = ray_tiles // len(parts)
    turns = ray_tiles // VG
    subset = subset_ref.shape[0]
    measured = ray_tiles + subset * turns
    total[...] = jnp.zeros_like(total)
    clear(operand, ray_tiles)
    for j, part in enumerate(parts):
        first = pl.multiple_of((slab ^ j) * own, own)
        sino[pl.ds(first, own), :] = part[pl.ds(measured, own), :]
        weight[pl.ds(first, own), :] = part[pl.ds(measured + own, own), :]
    row_sums = sum(part[pl.ds(0, ray_tiles), :] for part in parts)
    column = weight[pl.ds(0, ray_tiles), :] * row_sums
    fill(operand, 0, ray_tiles, ROWS, (column, jnp.zeros_like(column)))
    for j in range(subset):
        view = subset_ref[j]
        projected = sum(part[pl.ds(ray_tiles + j * turns, turns), :] for part in parts)
        rows = pl.ds(view, turns, stride=VG)
        residual = weight[rows, :] * (sino[rows, :] - projected)
        for at in (1, 3):
            operand[pl.ds(view * ROWS + at, turns, stride=ROWS * VG), :] = residual
    pad = packed(0, ray_tiles, total.shape[0] // ROWS - 1)
    slot_loop(list_ref, lengths(count_ref, ends_ref)[1], pad, tile_ref, operand, total, False)
    write_blocks(total, out_ref, 1)


def keep_kernel(list_ref, ends_ref, count_ref, operand, tile_ref, out_ref, total):
    total[...] = jnp.zeros_like(total)
    pad = packed(0, operand.shape[0] // ROWS - VG, total.shape[0] // ROWS - 1)
    slot_loop(list_ref, lengths(count_ref, ends_ref)[0], pad, tile_ref, operand, total, False)
    write_blocks(total, out_ref, 0)


def write_blocks(total, out_ref, odd):
    half, _, size, _ = out_ref.shape
    for j in range(half):
        for c in range(2):
            out_ref[j, c] = summed(total, (2 * j + odd) * size * ROWS + c, size, ROWS)


SMEM, VMEM, HBM = (pl.BlockSpec(memory_space=m) for m in (pltpu.SMEM, pltpu.VMEM, pltpu.HBM))
LIMIT = pltpu.CompilerParams(vmem_limit_bytes=16 << 20)


def call(kernel, name, inputs, outputs, scratch=(), aliases=None, cost=0):
    spaces = {pltpu.SMEM: SMEM, pltpu.VMEM: VMEM, pltpu.HBM: HBM}
    keys = [pltpu.SMEM if x.memory_space == pltpu.SMEM else pltpu.VMEM for x in outputs]
    return pl.pallas_call(
        kernel,
        out_shape=outputs,
        in_specs=[SMEM if m is None else spaces[m] for _, m in inputs],
        out_specs=[spaces[m] for m in keys],
        scratch_shapes=list(scratch),
        compiler_params=LIMIT,
        input_output_aliases=aliases or {},
        cost_estimate=pl.CostEstimate(flops=0, transcendentals=0, bytes_accessed=cost),
        name=name,
    )(*(x if m is None else pltpu.with_memory_space_constraint(x, m) for x, m in inputs))


def swap(x, axis, bit):
    return lax.ppermute(x, axis, [(i, i ^ bit) for i in range(lax.axis_size(axis))])


def bits(axis):
    return [1 << b for b in range(lax.axis_size(axis).bit_length() - 1)]


def on_device(volume, tile_blocks, pixel_tile, ray_tile, counts, subset_views, sinogram, weights):
    views, slabs = lax.axis_size("view"), lax.axis_size("slab")
    _, size, width = volume.shape
    slots, depth = tile_blocks.shape[2], tile_blocks.shape[3]
    own_rays = sinogram.shape[1]
    ray_tiles, voxel_tiles = own_rays * slabs, size * views
    turns = ray_tiles // VG
    sizes = dict(size=size, views=views)
    words = pltpu.SMEM((slots + BLOCKS[-1],), jnp.int32)
    assert max(slots, ray_tiles, voxel_tiles) < 1 << FIELD and slots % 8 == 0
    measured = pltpu.VMEM((own_rays, depth), jnp.float32)
    hbm = pltpu.HBM

    smem, vmem = pltpu.SMEM, pltpu.VMEM
    table = pltpu.SMEM((slots,), jnp.int32)
    ends = pltpu.SMEM((slots + 1,), jnp.int32)
    on_chip = pltpu.VMEM((slots, depth, width), jnp.bfloat16)
    view_bits = bits("view")
    arrived = swap(volume, "view", view_bits[0])
    pixel, ray, subset, sino, weight, image, tiles = call(
        first_kernel, "first",
        [(pixel_tile[0, 0], hbm), (ray_tile[0, 0], hbm), (subset_views[0], hbm),
         (sinogram[0], hbm), (weights[0], hbm), (volume, hbm), (tile_blocks[0, 0], hbm)],
        [table, table, pltpu.SMEM((subset_views.shape[1],), jnp.int32), measured, measured,
         pltpu.VMEM(volume.shape, jnp.float32), on_chip],
        [pltpu.SemaphoreType.DMA((6,)), pltpu.SemaphoreType.DMA((LOADS,))], cost=8 << 20,
    )
    for bit in view_bits[1:]:
        image = jnp.concatenate([image, arrived], axis=0)
        arrived = swap(image, "view", bit)
        if bit == view_bits[1]:
            early, late, forward_ends, image, tiles = call(
                lambda *refs: lists_kernel(*refs, **sizes), "lists",
                [(image, vmem), (pixel, smem), (ray, smem), (tile_blocks[0, 0], hbm), (tiles, vmem)],
                [words, words, ends, pltpu.VMEM(image.shape, jnp.float32), on_chip],
                [pltpu.SemaphoreType.DMA((LOADS,))], aliases={4: 4}, cost=8 << 20,
            )
    sums = pltpu.VMEM(((ray_tiles + VG) * ROWS, depth), jnp.float32)
    image_operand = pltpu.VMEM(((voxel_tiles + 1) * ROWS, width), jnp.float32)
    (total,) = call(
        early_kernel, "early",
        [(early, smem), (forward_ends, smem), (counts, None), (image, vmem), (tiles, vmem)],
        [sums], [image_operand], cost=8 << 20,
    )
    rows = ray_tiles + subset_views.shape[1] * turns + 2 * own_rays
    part, _ = call(
        late_kernel, "late",
        [(late, smem), (forward_ends, smem), (counts, None), (subset, smem), (arrived, vmem), (sino, vmem),
         (weight, vmem), (tiles, vmem), (total, vmem)],
        [pltpu.VMEM((rows, depth), jnp.float32), sums], [image_operand], aliases={8: 1},
    )
    parts = {0: part}
    for bit in reversed(bits("slab")):
        parts |= {j | bit: swap(p, "slab", bit) for j, p in parts.items()}
    keep_list, send_list, back_ends = call(
        lambda *refs: split_kernel(*refs, **sizes), "split",
        [(pixel, smem), (ray, smem), (part, vmem)], [words, words, ends],
        cost=4 << 20,
    )
    blocks = pltpu.VMEM((views // 2, 2, size, width), jnp.float32)
    back_sums = pltpu.VMEM(((voxel_tiles + 1) * ROWS, width), jnp.float32)
    rays = pltpu.VMEM((ray_tiles + VG, depth), jnp.float32)
    send, operand = call(
        send_kernel, "send",
        [(send_list, smem), (back_ends, smem), (counts, None), (subset, smem)]
        + [(parts[j], vmem) for j in range(slabs)] + [(tiles, vmem)],
        [blocks, sums], [back_sums, rays, rays],
    )
    (keep,) = call(
        keep_kernel, "keep",
        [(keep_list, smem), (back_ends, smem), (counts, None), (operand, vmem), (tiles, vmem)],
        [blocks], [back_sums], cost=8 << 20,
    )
    for bit in view_bits:
        both = keep + swap(send, "view", bit)
        keep, send = both[::2], both[1::2]
    denominators, gradient = keep[0, 0], keep[0, 1]
    updated = jnp.maximum(volume[0] + SUBSETS * gradient / denominators, 0.0)
    return (updated[None], denominators[None])


def solution(mesh):
    return jax.shard_map(
        on_device,
        mesh=mesh,
        in_specs=(
            P("slab", "view", None),
            P("view", "slab", None, None, None),
            P("view", "slab", None),
            P("view", "slab", None),
            P("view", "slab"),
            P("view", None),
            P("view", "slab", None),
            P("view", "slab", None),
        ),
        out_specs=(P("slab", "view", None), P("slab", "view", None)),
        check_vma=False,
    )
```

```python
import jax
import jax.numpy as jnp
from jax import lax
from jax.experimental import pallas as pl
from jax.experimental.pallas import tpu as pltpu
from jax.sharding import PartitionSpec as P

VG = 8
SUBSETS = 2
ROWS = 8
BLOCKS = 64, 16
LOADS = 8
EARLY_TILES = 45
FIELD = 10


def row_of(index):
    return pl.ds(pl.multiple_of(index * ROWS, ROWS), ROWS)


def relative(tile, size, me):
    if size & (size - 1) == 0:
        return tile ^ (me * size)
    return (lax.div(tile, size) ^ me) * size + lax.rem(tile, size)


def fill(operand, first, tiles, stride, columns):
    for c, column in enumerate(columns):
        for at in (c, c + 2):
            operand[pl.ds(first + at, tiles, stride=stride), :] = column


def packed(slot, ray, place):
    return slot | (ray << FIELD) | (place << (2 * FIELD))


def unpacked(word):
    mask = (1 << FIELD) - 1
    return word & mask, (word >> FIELD) & mask, word >> (2 * FIELD)


def make_lists(slots, pixel_ref, ray_ref, list_refs, ends_ref, choose, place_of):
    def body(step, ends):
        for u in range(8):
            k = step * 8 + u
            place = place_of(pixel_ref[k])
            word = packed(k, ray_ref[k], place)
            second = choose(place)
            ends_ref[k] = ends[1]
            for ref, end in zip(list_refs, ends):
                ref[end] = word
            ends = ends[0] + (1 - second), ends[1] + second
        return ends

    ends = lax.fori_loop(0, slots // 8, body, (jnp.int32(0), jnp.int32(0)))
    ends_ref[slots] = ends[1]


def lengths(count_ref, ends_ref):
    count = count_ref[0, 0]
    second = ends_ref[count]
    return count - second, second


def slot_loop(list_ref, length, pad, tile_ref, operand, total, forward):
    width = operand.shape[1]
    row = lax.broadcasted_iota(jnp.int32, (ROWS, width), 0)
    rows = row < 2, (row >= 2) & (row < 4)

    def block(first, size):
        for u in range(0, size, 2):
            pair = [list_ref[first + u + i] for i in range(2)]
            if size == BLOCKS[-1]:
                pair = [jnp.where(first + u + i < length, w, pad) for i, w in enumerate(pair)]
            pair = [unpacked(word) for word in pair]
            lhs = [
                jnp.where(mine, operand[row_of(place if forward else ray), :], 0.0)
                for (_, ray, place), mine in zip(pair, rows)
            ]
            lhs = jnp.concatenate(lhs, axis=1) if forward else lhs[0] + lhs[1]
            product = lax.dot_general(
                lhs.astype(jnp.bfloat16),
                jnp.concatenate([tile_ref[slot] for slot, _, _ in pair], axis=1),
                (((1,), (1 if forward else 0,)), ((), ())),
                preferred_element_type=jnp.float32,
            )
            for i, ((_, ray, place), mine) in enumerate(zip(pair, rows)):
                part = product if forward else product[:, i * width : (i + 1) * width]
                total[row_of(ray if forward else place), :] += jnp.where(mine, part, 0.0)

    done = jnp.int32(0)
    for size in BLOCKS:
        steps = lax.div(length - done + (size - 1 if size == BLOCKS[-1] else 0), size)

        def body(step, carry, done=done, size=size):
            block(done + step * size, size)
            return carry

        lax.fori_loop(0, steps, body, 0)
        done += steps * size


def summed(total, first, tiles, stride):
    return total[pl.ds(first, tiles, stride=stride), :] + total[pl.ds(first + 2, tiles, stride=stride), :]


def copy_all(pairs, sems):
    copies = [pltpu.make_async_copy(src, dst, sems.at[i]) for i, (src, dst) in enumerate(pairs)]
    for copy in copies:
        copy.start()
    return copies


def tile_copies(tiles_in, tiles_ref, sems, part):
    cut = tiles_in.shape[0] * EARLY_TILES // 100
    first, last = (0, cut) if part == 0 else (cut, tiles_in.shape[0])
    chunk = -(-(last - first) // LOADS)
    rows = [pl.ds(at, min(chunk, last - at)) for at in range(first, last, chunk)]
    return copy_all([(tiles_in.at[r], tiles_ref.at[r]) for r in rows], sems)


def first_kernel(*refs):
    half = (len(refs) - 2) // 2
    (*inputs, tiles_in), (*outputs, tiles_ref), (sems, tile_sems) = refs[:half], refs[half:-2], refs[-2:]
    pairs = [(src, dst if src.shape == dst.shape else dst.at[pl.ds(0, src.shape[0])]) for src, dst in zip(inputs, outputs)]
    copies = copy_all(pairs, sems)
    copies += tile_copies(tiles_in, tiles_ref, tile_sems, 0)
    for copy in copies:
        copy.wait()


def lists_kernel(
    image_in, pixel_ref, ray_ref, tiles_in, _, early_ref, late_ref, ends_ref, image_ref, tiles_ref, sems,
    *, size, views,
):
    me = lax.axis_index("view")
    copies = tile_copies(tiles_in, tiles_ref, sems, 1)
    image_ref[...] = image_in[...].astype(jnp.bfloat16)
    half = views * size // 2
    make_lists(
        pixel_ref.shape[0], pixel_ref, ray_ref, (early_ref, late_ref), ends_ref,
        lambda place: (place >= half).astype(jnp.int32), lambda tile: relative(tile, size, me),
    )
    for copy in copies:
        copy.wait()


def clear(ref, tiles):
    ref[row_of(tiles), :] = jnp.zeros((ROWS, ref.shape[1]), jnp.float32)


def rounded(image_ref):
    image = image_ref[...].astype(jnp.bfloat16).astype(jnp.float32)
    return image.reshape(-1, image.shape[-1])


def early_kernel(list_ref, ends_ref, count_ref, image_ref, tile_ref, total, operand):
    image = rounded(image_ref)
    tiles = image.shape[0]
    total[...] = jnp.zeros_like(total)
    clear(operand, 2 * tiles)
    fill(operand, 0, tiles, ROWS, (image, jnp.ones_like(image)))
    pad = packed(0, total.shape[0] // ROWS - VG, 2 * tiles)
    slot_loop(list_ref, lengths(count_ref, ends_ref)[0], pad, tile_ref, operand, total, True)


def late_kernel(
    list_ref, ends_ref, count_ref, subset_ref, image_ref, sino_ref, weight_ref, tile_ref, total_in,
    out_ref, total, operand,
):
    image = rounded(image_ref)
    tiles = image.shape[0]
    ray_tiles = total.shape[0] // ROWS - VG
    clear(operand, 2 * tiles)
    fill(operand, tiles * ROWS, tiles, ROWS, (image, jnp.ones_like(image)))
    pad = packed(0, ray_tiles, 2 * tiles)
    slot_loop(list_ref, lengths(count_ref, ends_ref)[1], pad, tile_ref, operand, total, True)
    out_ref[pl.ds(0, ray_tiles), :] = summed(total, 1, ray_tiles, ROWS)
    turns = ray_tiles // VG
    at = ray_tiles
    for j in range(subset_ref.shape[0]):
        first = pl.multiple_of(subset_ref[j] * ROWS, ROWS)
        out_ref[pl.ds(at, turns), :] = summed(total, first, turns, ROWS * VG)
        at += turns
    own = sino_ref.shape[0] - VG
    for j in range(subset_ref.shape[0]):
        out_ref[pl.ds(at, own // VG), :] = sino_ref[pl.ds(subset_ref[j], own // VG, stride=VG), :]
        at += own // VG
    out_ref[pl.ds(at, own), :] = weight_ref[pl.ds(0, own), :]


def prepare_kernel(
    pixel_ref, ray_ref, subset_ref, own_ref, near_ref,
    keep_ref, send_ref, ends_ref, sums_ref, operand, total, sino, weight, *, size, views, slabs,
):
    me, slab = lax.axis_index("view"), lax.axis_index("slab")
    make_lists(
        pixel_ref.shape[0], pixel_ref, ray_ref, (keep_ref, send_ref), ends_ref,
        lambda place: lax.div(place, size) & 1, lambda tile: relative(tile, size, me),
    )
    ray_tiles = operand.shape[0] // ROWS - VG
    total[...] = jnp.zeros_like(total)
    clear(operand, ray_tiles)
    empty = jnp.zeros((ray_tiles, operand.shape[1]), jnp.float32)
    for at in (1, 3):
        operand[pl.ds(at, ray_tiles, stride=ROWS), :] = empty
    sums_ref[...] = own_ref[pl.ds(0, sums_ref.shape[0]), :] + near_ref[pl.ds(0, sums_ref.shape[0]), :]
    for j, part in enumerate((own_ref, near_ref)):
        place_measured(part, slab ^ j, ray_tiles, slabs, subset_ref.shape[0], sino, weight)


def place_measured(part, slab, ray_tiles, slabs, subset, sino, weight):
    own, turns = ray_tiles // slabs, ray_tiles // VG
    at = ray_tiles + subset * turns
    for j in range(subset):
        sino[pl.ds(j * turns + slab * (own // VG), own // VG), :] = part[pl.ds(at, own // VG), :]
        at += own // VG
    weight[pl.ds(pl.multiple_of(slab * own, own), own), :] = part[pl.ds(at, own), :]


def send_kernel(list_ref, ends_ref, count_ref, subset_ref, *refs):
    *parts, tile_ref, sums_ref = refs[:-9]
    out_ref, operand, total, sino, weight = refs[-5:]
    slab = lax.axis_index("slab")
    ray_tiles = weight.shape[0] - VG
    turns, subset, slabs = ray_tiles // VG, subset_ref.shape[0], len(parts) + 2
    for j, part in enumerate(parts):
        place_measured(part, slab ^ (j + 2), ray_tiles, slabs, subset, sino, weight)

    def whole(first, tiles):
        rows = pl.ds(first, tiles)
        return sums_ref[rows, :] + sum(part[rows, :] for part in parts)

    column = weight[pl.ds(0, ray_tiles), :] * whole(0, ray_tiles)
    for at in (0, 2):
        operand[pl.ds(at, ray_tiles, stride=ROWS), :] = column
    for j in range(subset):
        view = subset_ref[j]
        projected = whole(ray_tiles + j * turns, turns)
        residual = weight[pl.ds(view, turns, stride=VG), :] * (sino[pl.ds(j * turns, turns), :] - projected)
        for at in (1, 3):
            operand[pl.ds(view * ROWS + at, turns, stride=ROWS * VG), :] = residual
    pad = packed(0, ray_tiles, total.shape[0] // ROWS - 1)
    slot_loop(list_ref, lengths(count_ref, ends_ref)[1], pad, tile_ref, operand, total, False)
    write_blocks(total, out_ref, 1)


def keep_kernel(list_ref, ends_ref, count_ref, operand, tile_ref, out_ref, total):
    total[...] = jnp.zeros_like(total)
    pad = packed(0, operand.shape[0] // ROWS - VG, total.shape[0] // ROWS - 1)
    slot_loop(list_ref, lengths(count_ref, ends_ref)[0], pad, tile_ref, operand, total, False)
    write_blocks(total, out_ref, 0)


def write_blocks(total, out_ref, odd):
    half, _, size, _ = out_ref.shape
    for j in range(half):
        for c in range(2):
            out_ref[j, c] = summed(total, (2 * j + odd) * size * ROWS + c, size, ROWS)


SMEM, VMEM, HBM = (pl.BlockSpec(memory_space=m) for m in (pltpu.SMEM, pltpu.VMEM, pltpu.HBM))
LIMIT = pltpu.CompilerParams(vmem_limit_bytes=16 << 20)


def call(kernel, name, inputs, outputs, scratch=(), aliases=None, cost=0):
    spaces = {pltpu.SMEM: SMEM, pltpu.VMEM: VMEM, pltpu.HBM: HBM}
    keys = [pltpu.SMEM if x.memory_space == pltpu.SMEM else pltpu.VMEM for x in outputs]
    return pl.pallas_call(
        kernel,
        out_shape=outputs,
        in_specs=[SMEM if m is None else spaces[m] for _, m in inputs],
        out_specs=[spaces[m] for m in keys],
        scratch_shapes=list(scratch),
        compiler_params=LIMIT,
        input_output_aliases=aliases or {},
        cost_estimate=pl.CostEstimate(flops=0, transcendentals=0, bytes_accessed=cost),
        name=name,
    )(*(x if m is None else pltpu.with_memory_space_constraint(x, m) for x, m in inputs))


def swap(x, axis, bit):
    return lax.ppermute(x, axis, [(i, i ^ bit) for i in range(lax.axis_size(axis))])


def bits(axis):
    return [1 << b for b in range(lax.axis_size(axis).bit_length() - 1)]


def on_device(volume, tile_blocks, pixel_tile, ray_tile, counts, subset_views, sinogram, weights):
    views, slabs = lax.axis_size("view"), lax.axis_size("slab")
    _, size, width = volume.shape
    slots, depth = tile_blocks.shape[2], tile_blocks.shape[3]
    own_rays = sinogram.shape[1]
    ray_tiles, voxel_tiles = own_rays * slabs, size * views
    turns = ray_tiles // VG
    sizes = dict(size=size, views=views)
    words = pltpu.SMEM((slots + BLOCKS[-1],), jnp.int32)
    assert max(slots, ray_tiles, voxel_tiles) < 1 << FIELD and slots % 8 == own_rays % VG == 0
    measured = pltpu.VMEM((own_rays + VG, depth), jnp.float32)
    hbm = pltpu.HBM

    smem, vmem = pltpu.SMEM, pltpu.VMEM
    table = pltpu.SMEM((slots,), jnp.int32)
    ends = pltpu.SMEM((slots + 1,), jnp.int32)
    on_chip = pltpu.VMEM((slots, depth, width), jnp.bfloat16)
    view_bits = bits("view")
    arrived = swap(volume, "view", view_bits[0])
    pixel, ray, subset, sino, weight, image, tiles = call(
        first_kernel, "first",
        [(pixel_tile[0, 0], hbm), (ray_tile[0, 0], hbm), (subset_views[0], hbm),
         (sinogram[0], hbm), (weights[0], hbm), (volume, hbm), (tile_blocks[0, 0], hbm)],
        [table, table, pltpu.SMEM((subset_views.shape[1],), jnp.int32), measured, measured,
         pltpu.VMEM(volume.shape, jnp.float32), on_chip],
        [pltpu.SemaphoreType.DMA((6,)), pltpu.SemaphoreType.DMA((LOADS,))], cost=8 << 20,
    )
    for bit in view_bits[1:]:
        image = jnp.concatenate([image, arrived.astype(image.dtype)], axis=0)
        if bit == view_bits[1]:
            image = lax.optimization_barrier(image)
        arrived = swap(image, "view", bit)
        if bit == view_bits[1]:
            early, late, forward_ends, image, tiles = call(
                lambda *refs: lists_kernel(*refs, **sizes), "lists",
                [(image, vmem), (pixel, smem), (ray, smem), (tile_blocks[0, 0], hbm), (tiles, vmem)],
                [words, words, ends, pltpu.VMEM(image.shape, jnp.bfloat16), on_chip],
                [pltpu.SemaphoreType.DMA((LOADS,))], aliases={4: 4}, cost=8 << 20,
            )
    sums = pltpu.VMEM(((ray_tiles + VG) * ROWS, depth), jnp.float32)
    image_operand = pltpu.VMEM(((voxel_tiles + 1) * ROWS, width), jnp.float32)
    (total,) = call(
        early_kernel, "early",
        [(early, smem), (forward_ends, smem), (counts, None), (image, vmem), (tiles, vmem)],
        [sums], [image_operand], cost=8 << 20,
    )
    rows = ray_tiles + subset_views.shape[1] * (turns + own_rays // VG) + own_rays
    part, _ = call(
        late_kernel, "late",
        [(late, smem), (forward_ends, smem), (counts, None), (subset, smem), (arrived, vmem), (sino, vmem),
         (weight, vmem), (tiles, vmem), (total, vmem)],
        [pltpu.VMEM((rows, depth), jnp.float32), sums], [image_operand], aliases={8: 1},
    )
    parts = {0: part}
    for bit in reversed(bits("slab")):
        parts |= {j | bit: swap(p, "slab", bit) for j, p in parts.items()}
    blocks = pltpu.VMEM((views // 2, 2, size, width), jnp.float32)
    back_sums = pltpu.VMEM(((voxel_tiles + 1) * ROWS, width), jnp.float32)
    rays = pltpu.VMEM((ray_tiles + VG, depth), jnp.float32)
    projected = pltpu.VMEM((ray_tiles + subset_views.shape[1] * turns, depth), jnp.float32)
    keep_list, send_list, back_ends, near, *prepared = call(
        lambda *refs: prepare_kernel(*refs, **sizes, slabs=slabs), "prepare",
        [(pixel, smem), (ray, smem), (subset, smem), (parts[0], vmem), (parts[1], vmem)],
        [words, words, ends, projected, sums, back_sums, rays, rays], cost=4 << 20,
    )
    send, operand, *_ = call(
        send_kernel, "send",
        [(send_list, smem), (back_ends, smem), (counts, None), (subset, smem)]
        + [(parts[j], vmem) for j in range(2, slabs)]
        + [(x, vmem) for x in (tiles, near, *prepared)],
        [blocks, sums, back_sums, rays, rays],
        aliases={slabs + 4 + i: 1 + i for i in range(4)},
    )
    (keep,) = call(
        keep_kernel, "keep",
        [(keep_list, smem), (back_ends, smem), (counts, None), (operand, vmem), (tiles, vmem)],
        [blocks], [back_sums], cost=8 << 20,
    )
    for bit in view_bits:
        both = keep + swap(send, "view", bit)
        keep, send = both[::2], both[1::2]
    denominators, gradient = keep[0, 0], keep[0, 1]
    updated = jnp.maximum(volume[0] + SUBSETS * gradient / denominators, 0.0)
    return (updated[None], denominators[None])


def solution(mesh):
    return jax.shard_map(
        on_device,
        mesh=mesh,
        in_specs=(
            P("slab", "view", None),
            P("view", "slab", None, None, None),
            P("view", "slab", None),
            P("view", "slab", None),
            P("view", "slab"),
            P("view", None),
            P("view", "slab", None),
            P("view", "slab", None),
        ),
        out_specs=(P("slab", "view", None), P("slab", "view", None)),
        check_vma=False,
    )
```
